1024 devices in a mesh: blk: 32 (over x, z_hi, core), trial: 4 (over z_lo), val: 8 (over y).
Axes of the slice: x: 8, y: 8, z: 8 (z_hi: 2, z_lo: 4; z = z_hi * 4 + z_lo), core: 2. Of those that a mesh axis runs over, the one named last changes fastest.
Arguments:
- trials: bfloat16 [32, 256, 512], P(None, None, 'trial'), may hold values from -6 to 6
- valence_factor: bfloat16 [512, 256, 256], P('blk', 'val'), may hold values from -0.015625 to 0.015625
- conduction_factor: bfloat16 [512, 512, 512], P('blk', 'trial'), may hold values from -0.25 to 0.25
- val_energy: float32 [256], P('val'), may hold values from -3 to -0.5
- cond_energy: float32 [512], P('trial'), may hold values from 0.5 to 3
Outputs:
- applied: float32 [32, 256, 512], P(None, 'val', 'trial')
- residual: float32 [32, 256, 512], P(None, 'val', 'trial')
- quotient: float32 [32], replicated
The draws below stay inside these ranges and needn't reach their ends.
All inputs are finite; a program needn't handle non-finite values.
Results may differ from the reference program's by a relative error of at most 0.002.
Values sent between devices are 32-bit elements; how exact they have to be, the bound alone decides.
A program may use at most 32 MiB of HBM per device.

```python
import jax
import jax.numpy as jnp
from jax import lax

NV = 256
NC = 512
TRIALS = 32
NAUX = 512


def shard_levels(rng, shape, pieces, low, high):
    loudness, own = 1.0, jax.random.fold_in(rng, 6)
    for axis_at, parts in pieces:
        draws = jnp.exp(jax.random.uniform(jax.random.fold_in(own, axis_at), (parts,), jnp.float32, low / len(pieces), high / len(pieces)))
        loudness = loudness * jnp.repeat(draws, shape[axis_at] // parts).reshape([-1 if axis == axis_at else 1 for axis in range(len(shape))])
    return loudness


def scatter_about(stream_key, shape, spread, most, cuts=(), held_as=jnp.bfloat16):
    drawn = spread * jax.random.normal(stream_key, shape, jnp.float32)
    if cuts:
        drawn = drawn * shard_levels(stream_key, shape, cuts, -0.22, 0.18)
    return jnp.clip(drawn, -most, most).astype(held_as)


def setup_inputs(seed: int = 0) -> dict:
    key_of = jax.random.split(jax.random.key(seed), 6)
    trials = scatter_about(key_of[0], (TRIALS, NV, NC), 1.0, 6.0, ((2, 4),))
    valence_factor = scatter_about(key_of[1], (NAUX, NV, NV), (NV * NAUX) ** -0.5, 0.015625, ((0, 32), (1, 8)))
    conduction_factor = scatter_about(key_of[2], (NAUX, NC, NC), NC ** -0.5, 0.25, ((0, 32), (1, 4)))
    val_energy = jnp.clip(-3.0 + 2.5 * jax.random.uniform(key_of[3], (NV,), jnp.float32) ** shard_levels(key_of[3], (NV,), ((0, 8),), -0.2, 0.2), -3.0, -0.5)
    cond_energy = jnp.clip(0.5 + 2.5 * jax.random.uniform(key_of[4], (NC,), jnp.float32) ** shard_levels(key_of[4], (NC,), ((0, 4),), -0.2, 0.2), 0.5, 3.0)
    return {"trials": trials, "valence_factor": valence_factor, "conduction_factor": conduction_factor, "val_energy": val_energy, "cond_energy": cond_energy}


def reference(trials, valence_factor, conduction_factor, val_energy, cond_energy):
    highest = lax.Precision.HIGHEST
    trial_values = trials.astype(jnp.float32)

    def one_function(totals, factors):
        valence_one, conduction_one = factors
        inner = jnp.einsum("vw,twc->tvc", valence_one.astype(jnp.float32), trial_values, precision=highest).astype(jnp.bfloat16)
        inner = lax.optimization_barrier(inner)
        added = jnp.einsum("tvc,cd->tvd", inner.astype(jnp.float32), conduction_one.astype(jnp.float32), precision=highest)
        return totals + added, None

    start_total = jnp.zeros(trials.shape, jnp.float32)
    direct, _ = lax.scan(one_function, start_total, (valence_factor, conduction_factor))
    energy = cond_energy[None, :] - val_energy[:, None]
    applied = direct + energy[None, :, :] * trial_values
    numerator = jnp.sum(trial_values * applied, axis=(1, 2))
    denominator = jnp.sum(trial_values * trial_values, axis=(1, 2)) + 1e-6
    quotient = numerator / denominator
    residual = applied - quotient[:, None, None] * trial_values
    return (applied, residual, quotient)
```

```python
import functools

import jax
import jax.numpy as jnp
from jax import lax
from jax.experimental import pallas as pl
from jax.experimental.pallas import tpu as pltpu
from jax.sharding import Mesh
from jax.sharding import PartitionSpec as P

BLK = ("x", "zh", "core")
MESH = pl.DeviceIdType.MESH
RING = 8
PAIR_ROWS = 64
SUBS = 4
SUB_ROWS = PAIR_ROWS // SUBS
TARGET = (4, 3, 5, 2, 6, 1, 7, 0)
SLOT_UP = (0, 1, 3, 5, 7)
SLOT_DOWN = (0, 2, 4, 6, 7)


def ring(i):
    return lax.rem(i, RING)


def kernel(
    trials_hbm, valence_hbm, conduction_hbm, energy_ref,
    applied_ref, residual_ref, quotient_ref,
    trials, valence, conduction, left, outgoing, from_core, own, from_x, blocks, from_z,
    gathered, sums, sums_z, sums_y, quotients,
    load_sem, core_send, core_recv, x_send, x_recv, z_send, z_recv, g_send, g_recv,
    f_send, f_recv, qz_send, qz_recv, qy_send, qy_recv, qx_send, qx_recv,
):
    x, zh, core = lax.axis_index("x"), lax.axis_index("zh"), lax.axis_index("core")
    zl, y = lax.axis_index("trial"), lax.axis_index("val")
    z = zh * 4 + zl
    other = 1 - core

    def at_x(step, c):
        return {"x": ring(x + step), "zh": zh, "core": c, "trial": zl, "val": y}

    def at_z(step):
        there = ring(z + step)
        return {"x": x, "zh": there // 4, "core": core, "trial": lax.rem(there, 4), "val": y}

    def at_y(step):
        return {"x": x, "zh": zh, "core": core, "trial": zl, "val": ring(y + step)}

    def remote(src, dst, send, recv, device):
        return pltpu.make_async_remote_copy(
            src_ref=src, dst_ref=dst, send_sem=send, recv_sem=recv,
            device_id=device, device_id_type=MESH,
        )

    loads = [
        pltpu.make_async_copy(valence_hbm, valence, load_sem.at[0]),
        pltpu.make_async_copy(trials_hbm, trials, load_sem.at[1]),
        pltpu.make_async_copy(conduction_hbm, conduction, load_sem.at[2]),
    ]
    for load in loads:
        load.start()
    barrier = pltpu.get_barrier_semaphore()
    partners = [at_x(0, other)]
    for step in range(1, RING):
        partners += [at_x(step, core), at_x(step, other), at_z(step), at_y(step)]
    for device in partners:
        pl.semaphore_signal(barrier, inc=1, device_id=device, device_id_type=MESH)
    loads[0].wait()
    loads[1].wait()

    def unit(half, u):
        for q in range(4):
            first = 16 * half + 2 * ring(x + TARGET[4 * u + q])
            pair = jnp.concatenate([trials[first], trials[first + 1]], axis=1)
            inner = jnp.dot(valence[...], pair, preferred_element_type=jnp.float32)
            inner = inner.astype(jnp.bfloat16)
            for p in range(16):
                for i in range(2):
                    left[q * 64 + i * 32:q * 64 + i * 32 + 32, p * 128:(p + 1) * 128] = (
                        inner[p * 32:(p + 1) * 32, i * 128:(i + 1) * 128]
                    )
        if half is other and u == 0:
            loads[2].wait()
        return jnp.dot(left[...], conduction[...], preferred_element_type=jnp.float32)

    to_core = []
    for u in range(2):
        outgoing[u] = unit(other, u)
        if u == 0:
            pl.semaphore_wait(barrier, len(partners))
        copy = remote(outgoing.at[u], from_core.at[u], core_send.at[u], core_recv.at[u],
                      at_x(0, other))
        copy.start()
        to_core.append(copy)

    x_copies = {}

    def send_x(way, hop, s):
        slot = (SLOT_UP, SLOT_DOWN)[way][hop]
        rows = pl.ds(s * SUB_ROWS, SUB_ROWS)
        copy = remote(own.at[slot, rows], from_x.at[way, hop, s], x_send.at[way, hop, s],
                      x_recv.at[way, hop, s], at_x((1, 7)[way], core))
        copy.start()
        x_copies[way, hop, s] = copy

    def long_chain(way, s):
        return (s < SUBS // 2) == (way == 0)

    for u in range(2):
        product = unit(core, u)
        to_core[u].wait_recv()
        for q in range(4):
            own[4 * u + q] = product[q * 64:(q + 1) * 64] + from_core[u, q * 64:(q + 1) * 64]
        if u == 0:
            for s in range(SUBS):
                for way in range(2):
                    if long_chain(way, s):
                        send_x(way, 0, s)
            for s in range(SUBS):
                for way in range(2):
                    if not long_chain(way, s):
                        send_x(way, 1, s)
    for turn in range(4):
        for s in range(SUBS):
            for way in range(2):
                hop = turn if long_chain(way, s) else turn + 1
                if hop > 3:
                    continue
                x_copies[way, hop, s].wait_recv()
                slot = (SLOT_UP, SLOT_DOWN)[way][hop + 1]
                rows = slice(s * SUB_ROWS, (s + 1) * SUB_ROWS)
                own[slot, rows] = own[slot, rows] + from_x[way, hop, s]
                if hop < 3:
                    send_x(way, hop + 1, s)

    for b in range(4):
        blocks[b] = own[7, :, b * 128:(b + 1) * 128]
    z_copies = {}
    for step in (4, 3, 5, 2, 6, 1, 7):
        block = lax.rem(zl + step, 4)
        copy = remote(blocks.at[block], from_z.at[step], z_send.at[step], z_recv.at[step], at_z(step))
        copy.start()
        z_copies[step] = copy
    from_z[0] = blocks[zl]
    for step in (1, 7, 2, 6, 3, 5, 4):
        z_copies[step].wait_recv()
    total = from_z[ring(z + RING)]
    for i in range(1, RING):
        total = total + from_z[ring(z + RING - i)]
    mine = core * 16 + x * 2
    v_rows = pl.ds(pl.multiple_of(y * 32, 32), 32)
    energy = energy_ref[...]
    products = []
    squares = []
    for i in range(2):
        vector = trials[mine + i, v_rows, :].astype(jnp.float32)
        image = total[i * 32:(i + 1) * 32] + energy * vector
        gathered[mine + i] = image
        products.append(jnp.sum(vector * image, axis=0, keepdims=True))
        squares.append(jnp.sum(vector * vector, axis=0, keepdims=True))
    sums_z[0] = jnp.concatenate(products + squares, axis=0)

    q_copies = []
    for step, slot in ((1, 3), (7, 1), (2, 2)):
        copy = remote(sums_z.at[0], sums_z.at[slot], qz_send.at[slot], qz_recv.at[slot], at_z(step))
        copy.start()
        q_copies.append(copy)
    g_copies = {}
    pair = pl.ds(mine, 2)
    for step in (4, 3, 5, 2, 6, 1, 7):
        copy = remote(gathered.at[pair], gathered.at[pair], g_send.at[step], g_recv.at[step],
                      at_x(step, core))
        copy.start()
        g_copies[step] = copy
    f_copies = {}

    def forward(step):
        there = pl.ds(core * 16 + 2 * ring(x + RING - step), 2)
        if step:
            g_copies[step].wait_recv()
        copy = remote(gathered.at[there], gathered.at[there], f_send.at[step], f_recv.at[step],
                      at_x(0, other))
        copy.start()
        f_copies[step] = copy

    forward(0)
    for copy in q_copies:
        copy.wait_recv()
    total = sums_z[lax.rem(4 - zl, 4)]
    for i in range(1, 4):
        total = total + sums_z[lax.rem(4 - zl + i, 4)]
    sums_y[0] = total
    y_copies = []
    for step in (4, 3, 5, 2, 6, 1, 7):
        copy = remote(sums_y.at[0], sums_y.at[step], qy_send.at[step], qy_recv.at[step], at_y(step))
        copy.start()
        y_copies.append(copy)
    for step in (1, 7, 2):
        forward(step)
    for copy in y_copies:
        copy.wait_recv()
    total = sums_y[ring(y + RING)]
    for i in range(1, RING):
        total = total + sums_y[ring(y + RING - i)]
    lanes = jnp.sum(total, axis=1, keepdims=True)
    ratio = lanes[0:2] / (lanes[2:4] + 1e-6)
    seat = core * 8 + x
    quotients[seat] = jnp.broadcast_to(ratio, (2, 128))
    for n in range(1, 16):
        step, c = n // 2, (core if n % 2 == 0 else other)
        copy = remote(quotients.at[seat], quotients.at[seat], qx_send.at[n], qx_recv.at[n], at_x(step, c))
        copy.start()
        q_copies.append(copy)
    for step in (6, 3, 5, 4):
        forward(step)
    for copy in q_copies[3:]:
        copy.wait_recv()
    for step in range(RING):
        f_copies[step].wait_recv()
    for n in range(16):
        for i in range(2):
            t = 2 * n + i
            row = quotients[n, i:i + 1, :]
            image = gathered[t]
            applied_ref[t] = image
            residual_ref[t] = image - row * trials[t, v_rows, :].astype(jnp.float32)
            quotient_ref[t:t + 1, :] = row
    for group in (to_core, x_copies.values(), z_copies.values(), g_copies.values(), f_copies.values(),
                  q_copies, y_copies):
        for copy in group:
            copy.wait_send()


def on_device(trials, valence_factor, conduction_factor, val_energy, cond_energy):
    energy = cond_energy[None, :] - val_energy[:, None]
    vmem = pl.BlockSpec(memory_space=pltpu.VMEM)
    hbm = pl.BlockSpec(memory_space=pl.ANY)
    dma = pltpu.SemaphoreType.DMA
    f32 = jnp.float32
    applied, residual, quotient = pl.pallas_call(
        kernel,
        out_shape=(
            jax.ShapeDtypeStruct((32, 32, 128), f32),
            jax.ShapeDtypeStruct((32, 32, 128), f32),
            jax.ShapeDtypeStruct((32, 128), f32),
        ),
        in_specs=[hbm, hbm, hbm, vmem],
        out_specs=(vmem, vmem, vmem),
        scratch_shapes=[
            pltpu.VMEM((32, 256, 128), jnp.bfloat16),
            pltpu.VMEM((512, 256), jnp.bfloat16),
            pltpu.VMEM((2048, 512), jnp.bfloat16),
            pltpu.VMEM((256, 2048), jnp.bfloat16),
            pltpu.VMEM((2, 256, 512), f32),
            pltpu.VMEM((2, 256, 512), f32),
            pltpu.VMEM((8, PAIR_ROWS, 512), f32),
            pltpu.VMEM((2, 4, SUBS, SUB_ROWS, 512), f32),
            pltpu.VMEM((4, PAIR_ROWS, 128), f32),
            pltpu.VMEM((8, PAIR_ROWS, 128), f32),
            pltpu.VMEM((32, 32, 128), f32),
            pltpu.VMEM((4, 128), f32),
            pltpu.VMEM((4, 4, 128), f32),
            pltpu.VMEM((8, 4, 128), f32),
            pltpu.VMEM((16, 2, 128), f32),
            dma((3,)), dma((2,)), dma((2,)), dma((2, 4, SUBS)), dma((2, 4, SUBS)),
            dma((8,)), dma((8,)), dma((8,)), dma((8,)), dma((8,)), dma((8,)),
            dma((4,)), dma((4,)), dma((8,)), dma((8,)), dma((16,)), dma((16,)),
        ],
        compiler_params=pltpu.CompilerParams(
            collective_id=0, has_side_effects=True, vmem_limit_bytes=56 * 1024 * 1024
        ),
        name="direct_term",
    )(trials, valence_factor.reshape(512, 256), conduction_factor.reshape(2048, 512), energy)
    return (applied, residual, quotient[:, 0])


def solution(mesh):
    split = Mesh(
        mesh.devices.reshape(8, 2, 2, mesh.shape["trial"], mesh.shape["val"]),
        ("x", "zh", "core", "trial", "val"),
    )
    in_specs = (P(None, None, "trial"), P(BLK, "val", None), P(BLK, "trial", None), P("val"), P("trial"))
    out_specs = (P(None, "val", "trial"), P(None, "val", "trial"), P())
    return jax.shard_map(on_device, mesh=split, in_specs=in_specs, out_specs=out_specs, check_vma=False)
```

```python
import functools

import jax
import jax.numpy as jnp
from jax import lax
from jax.experimental import pallas as pl
from jax.experimental.pallas import tpu as pltpu
from jax.sharding import Mesh
from jax.sharding import PartitionSpec as P

BLK = ("x", "zh", "core")
MESH = pl.DeviceIdType.MESH
RING = 8
PAIR_ROWS = 64
SUBS = 4
SUB_ROWS = PAIR_ROWS // SUBS
TARGET = (4, 3, 5, 2, 6, 1, 7, 0)
SLOT_UP = (0, 1, 3, 5, 7)
SLOT_DOWN = (0, 2, 4, 6, 7)


def ring(i):
    return lax.rem(i, RING)


def kernel(
    trials, valence, conduction, val_ref, cond_ref,
    applied_ref, residual_ref, quotient_ref,
    left, outgoing, from_core, own, from_x, blocks, from_z,
    gathered, vectors, sums_y, sums_z, quotients,
    core_send, core_recv, x_send, x_recv, z_send, z_recv, g_send, g_recv,
    f_send, f_recv, t_send, t_recv, qy_send, qy_recv, qz_send, qz_recv, qx_send, qx_recv,
):
    x, zh, core = lax.axis_index("x"), lax.axis_index("zh"), lax.axis_index("core")
    zl, y = lax.axis_index("trial"), lax.axis_index("val")
    z = zh * 4 + zl
    other = 1 - core

    def at_x(step, c):
        return {"x": ring(x + step), "zh": zh, "core": c, "trial": zl, "val": y}

    def at_z(step):
        there = ring(z + step)
        return {"x": x, "zh": there // 4, "core": core, "trial": lax.rem(there, 4), "val": y}

    def at_y(step):
        return {"x": x, "zh": zh, "core": core, "trial": zl, "val": ring(y + step)}

    def remote(src, dst, send, recv, device):
        return pltpu.make_async_remote_copy(
            src_ref=src, dst_ref=dst, send_sem=send, recv_sem=recv,
            device_id=device, device_id_type=MESH,
        )

    barrier = pltpu.get_barrier_semaphore()
    partners = [at_x(0, other)]
    for step in range(1, RING):
        partners += [at_x(step, core), at_x(step, other), at_z(step), at_y(step)]
    for device in partners:
        pl.semaphore_signal(barrier, inc=1, device_id=device, device_id_type=MESH)

    def unit(half, u):
        for q in range(4):
            first = 16 * half + 2 * ring(x + TARGET[4 * u + q])
            pair = jnp.concatenate([trials[first], trials[first + 1]], axis=1)
            inner = jnp.dot(valence[...], pair, preferred_element_type=jnp.float32)
            inner = inner.astype(jnp.bfloat16)
            for p in range(16):
                for i in range(2):
                    left[q * 64 + i * 32:q * 64 + i * 32 + 32, p * 128:(p + 1) * 128] = (
                        inner[p * 32:(p + 1) * 32, i * 128:(i + 1) * 128]
                    )
        return jnp.dot(left[...], conduction[...], preferred_element_type=jnp.float32)

    mine = core * 16 + x * 2
    v_rows = pl.ds(pl.multiple_of(y * 32, 32), 32)
    for i in range(2):
        vectors[0, i * 32:(i + 1) * 32] = trials[mine + i, v_rows, :].astype(jnp.float32)
    small = []
    to_core = []

    def exchange(u):
        outgoing[u] = unit(other, u)
        if u == 0:
            pl.semaphore_wait(barrier, len(partners))
        copy = remote(outgoing.at[u], from_core.at[u], core_send.at[u], core_recv.at[u],
                      at_x(0, other))
        copy.start()
        to_core.append(copy)

    x_copies = {}

    def send_x(way, hop, s):
        slot = (SLOT_UP, SLOT_DOWN)[way][hop]
        rows = pl.ds(s * SUB_ROWS, SUB_ROWS)
        copy = remote(own.at[slot, rows], from_x.at[way, hop, s], x_send.at[way, hop, s],
                      x_recv.at[way, hop, s], at_x((1, 7)[way], core))
        copy.start()
        x_copies[way, hop, s] = copy

    def long_chain(way, s):
        return (s < SUBS // 2) == (way == 0)

    for u in range(2):
        exchange(u)
        if u == 0:
            for step, slot in ((1, 3), (7, 1), (2, 2)):
                copy = remote(vectors.at[0], vectors.at[slot], t_send.at[slot], t_recv.at[slot], at_z(step))
                copy.start()
                small.append(copy)
        product = unit(core, u)
        to_core[u].wait_recv()
        for q in range(4):
            own[4 * u + q] = product[q * 64:(q + 1) * 64] + from_core[u, q * 64:(q + 1) * 64]
        if u == 0:
            for s in range(SUBS):
                for way in range(2):
                    if long_chain(way, s):
                        send_x(way, 0, s)
            for s in range(SUBS):
                for way in range(2):
                    if not long_chain(way, s):
                        send_x(way, 1, s)
    for turn in range(4):
        for s in range(SUBS):
            for way in range(2):
                hop = turn if long_chain(way, s) else turn + 1
                if hop > 3:
                    continue
                x_copies[way, hop, s].wait_recv()
                slot = (SLOT_UP, SLOT_DOWN)[way][hop + 1]
                rows = slice(s * SUB_ROWS, (s + 1) * SUB_ROWS)
                own[slot, rows] = own[slot, rows] + from_x[way, hop, s]
                if hop < 3:
                    send_x(way, hop + 1, s)

    for b in range(4):
        blocks[b] = own[7, :, b * 128:(b + 1) * 128]
    z_copies = {}
    for step in (4, 3, 5, 2, 6, 1, 7):
        block = lax.rem(zl + step, 4)
        copy = remote(blocks.at[block], from_z.at[step], z_send.at[step], z_recv.at[step], at_z(step))
        copy.start()
        z_copies[step] = copy
    from_z[0] = blocks[zl]

    def slot_of(block):
        return lax.rem(block + 4 - zl, 4)

    seat_rows = lax.broadcasted_iota(jnp.int32, (32, 32), 0) == lax.broadcasted_iota(jnp.int32, (32, 32), 1)
    val = jnp.sum(jnp.where(seat_rows, jnp.broadcast_to(val_ref[...], (32, 32)), 0.0), axis=1, keepdims=True)
    energy = cond_ref[...] - val
    for copy in small:
        copy.wait_recv()
    products, squares = [], []
    for i in range(2):
        rows = slice(i * 32, (i + 1) * 32)
        product = vectors[slot_of(0), rows] * own[7, rows, 0:128]
        for b in range(1, 4):
            product = product + vectors[slot_of(b), rows] * own[7, rows, b * 128:(b + 1) * 128]
        square = jnp.where(zh == 0, vectors[0, rows] * vectors[0, rows], 0.0)
        product = product + energy * square
        products.append(jnp.sum(product, axis=0, keepdims=True))
        squares.append(jnp.sum(square, axis=0, keepdims=True))
    sums_y[0] = jnp.concatenate(products + squares, axis=0)
    y_copies = []
    for step in (4, 3, 5, 2, 6, 1, 7):
        copy = remote(sums_y.at[0], sums_y.at[step], qy_send.at[step], qy_recv.at[step], at_y(step))
        copy.start()
        y_copies.append(copy)
    for copy in y_copies:
        copy.wait_recv()
    total = sums_y[ring(y + RING)]
    for i in range(1, RING):
        total = total + sums_y[ring(y + RING - i)]
    sums_z[0] = total
    q_copies = []
    for step in (4, 3, 5, 2, 6, 1, 7):
        copy = remote(sums_z.at[0], sums_z.at[step], qz_send.at[step], qz_recv.at[step], at_z(step))
        copy.start()
        q_copies.append(copy)

    for step in (1, 7, 2, 6, 3, 5, 4):
        z_copies[step].wait_recv()
    total = from_z[ring(z + RING)]
    for i in range(1, RING):
        total = total + from_z[ring(z + RING - i)]
    for i in range(2):
        rows = slice(i * 32, (i + 1) * 32)
        gathered[mine + i] = total[rows] + energy * vectors[0, rows]
    g_copies = {}
    pair = pl.ds(mine, 2)
    for step in (4, 3, 5, 2, 6, 1, 7):
        copy = remote(gathered.at[pair], gathered.at[pair], g_send.at[step], g_recv.at[step],
                      at_x(step, core))
        copy.start()
        g_copies[step] = copy
    f_copies = {}

    def forward(step):
        there = pl.ds(core * 16 + 2 * ring(x + RING - step), 2)
        if step:
            g_copies[step].wait_recv()
        copy = remote(gathered.at[there], gathered.at[there], f_send.at[step], f_recv.at[step],
                      at_x(0, other))
        copy.start()
        f_copies[step] = copy

    for step in (0, 1, 7):
        forward(step)
    for copy in q_copies:
        copy.wait_recv()
    total = sums_z[ring(z + RING)]
    for i in range(1, RING):
        total = total + sums_z[ring(z + RING - i)]
    lanes = jnp.sum(total, axis=1, keepdims=True)
    ratio = lanes[0:2] / (lanes[2:4] + 1e-6)
    seat = core * 8 + x
    quotients[seat] = jnp.broadcast_to(ratio, (2, 128))
    seat_copies = []
    for n in range(2, 16):
        step, c = n // 2, (core if n % 2 == 0 else other)
        copy = remote(quotients.at[seat], quotients.at[seat], qx_send.at[n], qx_recv.at[n], at_x(step, c))
        copy.start()
        seat_copies.append(copy)
    copy = remote(quotients.at[seat], quotients.at[seat], qx_send.at[1], qx_recv.at[1], at_x(0, other))
    copy.start()
    seat_copies.append(copy)
    for step in (2, 6, 3, 5, 4):
        forward(step)
    for step in range(RING):
        f_copies[step].wait_recv()
    applied_ref[...] = gathered[...]
    for copy in seat_copies:
        copy.wait_recv()
    lane = lax.broadcasted_iota(jnp.int32, (1, 128), 1)
    everyone = jnp.zeros((1, 128), jnp.float32)
    for n in range(16):
        for i in range(2):
            t = 2 * n + i
            row = quotients[n, i:i + 1, :]
            residual_ref[t] = gathered[t] - row * trials[t, v_rows, :].astype(jnp.float32)
            everyone = jnp.where(lane == t, row, everyone)
    quotient_ref[...] = everyone[:, 0:32]
    for group in (to_core, x_copies.values(), z_copies.values(), g_copies.values(), f_copies.values(),
                  small, y_copies, q_copies, seat_copies):
        for copy in group:
            copy.wait_send()


def on_device(trials, valence_factor, conduction_factor, val_energy, cond_energy):
    vmem = pl.BlockSpec(memory_space=pltpu.VMEM)
    dma = pltpu.SemaphoreType.DMA
    f32 = jnp.float32
    applied, residual, quotient = pl.pallas_call(
        kernel,
        out_shape=(
            jax.ShapeDtypeStruct((32, 32, 128), f32),
            jax.ShapeDtypeStruct((32, 32, 128), f32),
            jax.ShapeDtypeStruct((1, 32), f32),
        ),
        in_specs=[vmem] * 5,
        out_specs=(vmem, vmem, vmem),
        scratch_shapes=[
            pltpu.VMEM((256, 2048), jnp.bfloat16),
            pltpu.VMEM((2, 256, 512), f32),
            pltpu.VMEM((2, 256, 512), f32),
            pltpu.VMEM((8, PAIR_ROWS, 512), f32),
            pltpu.VMEM((2, 4, SUBS, SUB_ROWS, 512), f32),
            pltpu.VMEM((4, PAIR_ROWS, 128), f32),
            pltpu.VMEM((8, PAIR_ROWS, 128), f32),
            pltpu.VMEM((32, 32, 128), f32),
            pltpu.VMEM((4, PAIR_ROWS, 128), f32),
            pltpu.VMEM((8, 4, 128), f32),
            pltpu.VMEM((8, 4, 128), f32),
            pltpu.VMEM((16, 2, 128), f32),
            dma((2,)), dma((2,)), dma((2, 4, SUBS)), dma((2, 4, SUBS)),
            dma((8,)), dma((8,)), dma((8,)), dma((8,)), dma((8,)), dma((8,)),
            dma((4,)), dma((4,)), dma((8,)), dma((8,)), dma((8,)), dma((8,)), dma((16,)), dma((16,)),
        ],
        compiler_params=pltpu.CompilerParams(
            collective_id=0, has_side_effects=True, vmem_limit_bytes=32 * 1024 * 1024
        ),
        name="direct_term",
    )(trials, valence_factor.reshape(512, 256), conduction_factor.reshape(2048, 512),
      val_energy.reshape(1, 32), cond_energy.reshape(1, 128))
    return (applied, residual, quotient.reshape(32))


def solution(mesh):
    split = Mesh(
        mesh.devices.reshape(8, 2, 2, mesh.shape["trial"], mesh.shape["val"]),
        ("x", "zh", "core", "trial", "val"),
    )
    in_specs = (P(None, None, "trial"), P(BLK, "val", None), P(BLK, "trial", None), P("val"), P("trial"))
    out_specs = (P(None, "val", "trial"), P(None, "val", "trial"), P())
    return jax.shard_map(on_device, mesh=split, in_specs=in_specs, out_specs=out_specs, check_vma=False)
```

```python
import jax
import jax.numpy as jnp
from jax import lax
from jax.experimental import pallas as pl
from jax.experimental.pallas import tpu as pltpu
from jax.sharding import Mesh
from jax.sharding import PartitionSpec as P

BLK = ("x", "zh", "core")
MESH = pl.DeviceIdType.MESH
RING = 8
PAIR_ROWS = 64
TARGET = (4, 3, 5, 2, 6, 1, 7, 0)
FAR_FIRST = (4, 3, 5, 2, 6, 1, 7)


def ring(i):
    return lax.rem(i, RING)


def kernel(
    trials_hbm, valence_hbm, conduction_hbm, val_hbm, cond_hbm,
    applied_ref, residual_ref, quotient_ref,
    trials, valence, conduction, val_ref, cond_ref, left, outgoing, from_core, own,
    from_4, from_3, from_2, from_1, blocks, from_z, vectors,
    below, above, beyond, part, from_x, half, other_half, whole,
    gathered, sums_y, sums_z, sums_x,
    load_sem, core_send, core_recv, a_send, a_recv, z_send, z_recv, t_send, t_recv,
    b_send, b_recv, x_send, x_recv, h_send, h_recv, g_send, g_recv, f_send, f_recv,
    qy_send, qy_recv, qz_send, qz_recv, qx_send, qx_recv,
):
    x, zh, core = lax.axis_index("x"), lax.axis_index("zh"), lax.axis_index("core")
    zl, y = lax.axis_index("trial"), lax.axis_index("val")
    z = zh * 4 + zl
    other = 1 - core

    def at_x(step, c):
        return {"x": ring(x + step), "zh": zh, "core": c, "trial": zl, "val": y}

    def at_z(step):
        there = ring(z + step)
        return {"x": x, "zh": there // 4, "core": core, "trial": lax.rem(there, 4), "val": y}

    def at_y(step):
        return {"x": x, "zh": zh, "core": core, "trial": zl, "val": ring(y + step)}

    def remote(src, dst, send, recv, device):
        return pltpu.make_async_remote_copy(
            src_ref=src, dst_ref=dst, send_sem=send, recv_sem=recv,
            device_id=device, device_id_type=MESH,
        )

    loads = [
        pltpu.make_async_copy(src, dst, load_sem.at[i])
        for i, (src, dst) in enumerate((
            (valence_hbm, valence), (trials_hbm, trials), (conduction_hbm, conduction),
            (val_hbm, val_ref), (cond_hbm, cond_ref),
        ))
    ]
    for load in loads:
        load.start()
    barrier = pltpu.get_barrier_semaphore()
    partners = [at_x(0, other)]
    for step in range(1, RING):
        partners += [at_x(step, core), at_x(step, other), at_z(step), at_y(step)]
    for device in partners:
        pl.semaphore_signal(barrier, inc=1, device_id=device, device_id_type=MESH)
    loads[0].wait()
    loads[1].wait()

    def unit(side, u):
        for q in range(4):
            first = 16 * side + 2 * ring(x + TARGET[4 * u + q])
            pair = jnp.concatenate([trials[first], trials[first + 1]], axis=1)
            inner = jnp.dot(valence[...], pair, preferred_element_type=jnp.float32)
            inner = inner.astype(jnp.bfloat16)
            for p in range(16):
                for i in range(2):
                    left[q * 64 + i * 32:q * 64 + i * 32 + 32, p * 128:(p + 1) * 128] = (
                        inner[p * 32:(p + 1) * 32, i * 128:(i + 1) * 128]
                    )
        if side is other and u == 0:
            loads[2].wait()
        return jnp.dot(left[...], conduction[...], preferred_element_type=jnp.float32)

    mine = core * 16 + x * 2
    v_rows = pl.ds(pl.multiple_of(y * 32, 32), 32)
    for i in range(2):
        vectors[0, i * 32:(i + 1) * 32] = trials[mine + i, v_rows, :].astype(jnp.float32)

    def trial_copies():
        return [
            remote(vectors.at[0], vectors.at[slot], t_send.at[slot], t_recv.at[slot], at_z(step))
            for step, slot in ((1, 3), (7, 1), (2, 2))
        ]

    def along_x(kind, way):
        n = kind * 2 + way
        send, recv = a_send.at[n], a_recv.at[n]
        if kind == 0:
            src, dst = own.at[0, pl.ds(32 * way, 32)], from_4.at[way]
        else:
            slot = ((1, 2), (3, 4), (5, 6))[kind - 1][way]
            src, dst = own.at[slot], (from_3, from_2, from_1)[kind - 1].at[way]
        reach = (2, 1, 2, 1)[kind]
        return remote(src, dst, send, recv, at_x((reach, RING - reach)[way], core))

    def block_of(step, u):
        column = pl.multiple_of(lax.rem(zl + step, 4) * 128, 128)
        return own.at[pl.ds(4 * u, 4), pl.ds(0, PAIR_ROWS), pl.ds(column, 128)]

    def along_z(u):
        far = (2, 6)[u]
        return [
            remote(block_of(far, u), beyond.at[u], b_send.at[4 + u], b_recv.at[4 + u], at_z(far)),
            remote(block_of(1, u), below.at[u], b_send.at[u], b_recv.at[u], at_z(1)),
            remote(block_of(7, u), above.at[u], b_send.at[2 + u], b_recv.at[2 + u], at_z(7)),
        ]

    to_core = []
    for u in range(2):
        outgoing[u] = unit(other, u)
        if u == 0:
            pl.semaphore_wait(barrier, len(partners))
        copy = remote(outgoing.at[u], from_core.at[u], core_send.at[u], core_recv.at[u], at_x(0, other))
        copy.start()
        to_core.append(copy)
        if u == 0:
            @pl.when(core == 0)
            def _():
                for copy in trial_copies():
                    copy.start()
        product = unit(core, u)
        to_core[u].wait_recv()
        for q in range(4):
            own[4 * u + q] = product[q * 64:(q + 1) * 64] + from_core[u, q * 64:(q + 1) * 64]

        @pl.when(core == 0)
        def _():
            if u == 0:
                for kind in (0, 1):
                    for way in range(2):
                        along_x(kind, way).start()
            else:
                for way in range(2):
                    along_x(0, way).wait_recv()
                    along_x(1, way).wait_recv()
                    slot, rows = 3 + way, slice(32 * way, 32 * way + 32)
                    own[slot] = own[slot] + from_3[way]
                    own[slot, rows] = own[slot, rows] + from_4[way]
                    along_x(2, way).start()
                for way in range(2):
                    along_x(3, way).start()

        @pl.when(core == 1)
        def _():
            for copy in along_z(u):
                copy.start()

    loads[3].wait()
    loads[4].wait()
    on_diagonal = lax.broadcasted_iota(jnp.int32, (32, 128), 0) == lax.broadcasted_iota(jnp.int32, (32, 128), 1)
    val_row = jnp.concatenate([val_ref[...], jnp.zeros((1, 96), jnp.float32)], axis=1)
    energy = cond_ref[...] - jnp.sum(jnp.where(on_diagonal, val_row, 0.0), axis=1, keepdims=True)

    def in_lanes(values, first):
        count = values.shape[0]
        column = jnp.sum(values, axis=1, keepdims=True)
        lane = lax.broadcasted_iota(jnp.int32, (count, 128), 1)
        row = lax.broadcasted_iota(jnp.int32, (count, 128), 0)
        return jnp.sum(jnp.where(lane == row + first, column, 0.0), axis=0, keepdims=True)

    def over_rows(values):
        return jnp.sum(values, axis=0, keepdims=True)

    fixed, squares = [], []
    for i in range(2):
        vector = vectors[0, i * 32:(i + 1) * 32]
        square = jnp.where(zh == 0, vector * vector, 0.0)
        fixed.append(over_rows(energy * square))
        squares.append(over_rows(square))
    fixed = in_lanes(jnp.concatenate(fixed, axis=0), mine)
    sums_y[0, 1:2] = in_lanes(jnp.concatenate(squares, axis=0), mine)

    def z_copy(step):
        return remote(blocks.at[lax.rem(zl + step, 4)], from_z.at[step], z_send.at[step], z_recv.at[step], at_z(step))

    def x_copy(step):
        return remote(part.at[ring(x + step)], from_x.at[step], x_send.at[step], x_recv.at[step], at_x(step, core))

    def half_copy():
        return remote(half, other_half, h_send.at[0], h_recv.at[0], at_z(4))

    @pl.when(core == 0)
    def _():
        for kind in (3, 2):
            for way in range(2):
                along_x(kind, way).wait_recv()
        summed = own[7] + from_1[0] + from_1[1] + from_2[0] + from_2[1]
        for b in range(4):
            blocks[b] = summed[:, b * 128:(b + 1) * 128]
        for step in FAR_FIRST:
            z_copy(step).start()
        from_z[0] = blocks[zl]
        for copy in trial_copies():
            copy.wait_recv()
        products = []
        for i in range(2):
            rows = slice(i * 32, (i + 1) * 32)
            product = vectors[0, rows] * blocks[zl, rows]
            for b in range(1, 4):
                product = product + vectors[b, rows] * blocks[lax.rem(zl + b, 4), rows]
            products.append(over_rows(product))
        sums_y[0, 0:1] = fixed + in_lanes(jnp.concatenate(products, axis=0), mine)

    @pl.when(core == 1)
    def _():
        products = [None] * 16
        column = pl.ds(pl.multiple_of(zl * 128, 128), 128)
        for u in range(2):
            for copy in along_z(u):
                copy.wait_recv()
            for q in range(4):
                k = 4 * u + q
                part[ring(x + TARGET[k])] = own[k, :, column] + below[u, q] + above[u, q] + beyond[u, q]
        for step in FAR_FIRST:
            x_copy(step).start()
        for t in range(16):
            image = part[t // 2, (t % 2) * 32:(t % 2) * 32 + 32]
            products[t] = over_rows(image * trials[16 + t, v_rows, :].astype(jnp.float32))
        sums_y[0, 0:1] = fixed + in_lanes(jnp.concatenate(products, axis=0), 16)

    y_copies = []
    for step in FAR_FIRST:
        copy = remote(sums_y.at[0], sums_y.at[step], qy_send.at[step], qy_recv.at[step], at_y(step))
        copy.start()
        y_copies.append(copy)
    for copy in y_copies:
        copy.wait_recv()
    total = sums_y[ring(y + RING)]
    for i in range(1, RING):
        total = total + sums_y[ring(y + RING - i)]
    sums_z[0] = total
    q_copies = []
    for step in FAR_FIRST:
        copy = remote(sums_z.at[0], sums_z.at[step], qz_send.at[step], qz_recv.at[step], at_z(step))
        copy.start()
        q_copies.append(copy)

    @pl.when(core == 0)
    def _():
        for step in reversed(FAR_FIRST):
            z_copy(step).wait_recv()
        total = from_z[ring(z + RING)]
        for i in range(1, RING):
            total = total + from_z[ring(z + RING - i)]
        whole[...] = total

    @pl.when(core == 1)
    def _():
        total = part[x]
        for step in reversed(FAR_FIRST):
            x_copy(step).wait_recv()
            total = total + from_x[step]
        half[...] = total
        half_copy().start()
        half_copy().wait_recv()
        whole[...] = half[...] + other_half[...]

    for i in range(2):
        rows = slice(i * 32, (i + 1) * 32)
        gathered[mine + i] = whole[rows] + energy * vectors[0, rows]
    g_copies = {}
    pair = pl.ds(mine, 2)
    for step in FAR_FIRST:
        copy = remote(gathered.at[pair], gathered.at[pair], g_send.at[step], g_recv.at[step], at_x(step, core))
        copy.start()
        g_copies[step] = copy
    f_copies = {}

    def forward(step):
        there = pl.ds(core * 16 + 2 * ring(x + RING - step), 2)
        if step:
            g_copies[step].wait_recv()
        copy = remote(gathered.at[there], gathered.at[there], f_send.at[step], f_recv.at[step], at_x(0, other))
        copy.start()
        f_copies[step] = copy

    forward(0)
    for copy in q_copies:
        copy.wait_recv()
    total = sums_z[ring(z + RING)]
    for i in range(1, RING):
        total = total + sums_z[ring(z + RING - i)]
    seat = core * 8 + x
    sums_x[seat] = total
    seat_copies = []
    for n in list(range(2, 16)) + [1]:
        step, c = n // 2, (core if n % 2 == 0 else other)
        copy = remote(sums_x.at[seat], sums_x.at[seat], qx_send.at[n], qx_recv.at[n], at_x(step, c))
        copy.start()
        seat_copies.append(copy)
    for step in reversed(FAR_FIRST):
        forward(step)
    for copy in seat_copies:
        copy.wait_recv()
    total = sums_x[0]
    for n in range(1, 16):
        total = total + sums_x[n]
    ratio = total[0:1] / (total[1:2] + 1e-6)
    quotient_ref[...] = ratio[:, 0:32]
    quotients = jnp.sum(jnp.where(on_diagonal, ratio, 0.0), axis=1, keepdims=True)
    for step in range(RING):
        f_copies[step].wait_recv()
    for t in range(32):
        image = gathered[t]
        applied_ref[t] = image
        residual_ref[t] = image - quotients[t:t + 1, :] * trials[t, v_rows, :].astype(jnp.float32)

    @pl.when(core == 0)
    def _():
        for copy in trial_copies():
            copy.wait_send()
        for kind in range(4):
            for way in range(2):
                along_x(kind, way).wait_send()
        for step in FAR_FIRST:
            z_copy(step).wait_send()

    @pl.when(core == 1)
    def _():
        for u in range(2):
            for copy in along_z(u):
                copy.wait_send()
        for step in FAR_FIRST:
            x_copy(step).wait_send()
        half_copy().wait_send()

    for group in (to_core, g_copies.values(), f_copies.values(), y_copies, q_copies, seat_copies):
        for copy in group:
            copy.wait_send()


def on_device(trials, valence_factor, conduction_factor, val_energy, cond_energy):
    vmem = pl.BlockSpec(memory_space=pltpu.VMEM)
    hbm = pl.BlockSpec(memory_space=pltpu.HBM)
    dma = pltpu.SemaphoreType.DMA
    f32 = jnp.float32
    applied, residual, quotient = pl.pallas_call(
        kernel,
        out_shape=(
            jax.ShapeDtypeStruct((32, 32, 128), f32),
            jax.ShapeDtypeStruct((32, 32, 128), f32),
            jax.ShapeDtypeStruct((1, 32), f32),
        ),
        in_specs=[hbm] * 5,
        out_specs=(vmem, vmem, vmem),
        scratch_shapes=[
            pltpu.VMEM((32, 256, 128), jnp.bfloat16),
            pltpu.VMEM((512, 256), jnp.bfloat16),
            pltpu.VMEM((2048, 512), jnp.bfloat16),
            pltpu.VMEM((1, 32), f32),
            pltpu.VMEM((1, 128), f32),
            pltpu.VMEM((256, 2048), jnp.bfloat16),
            pltpu.VMEM((2, 256, 512), f32),
            pltpu.VMEM((2, 256, 512), f32),
            pltpu.VMEM((8, PAIR_ROWS, 512), f32),
            pltpu.VMEM((2, 32, 512), f32),
            pltpu.VMEM((2, PAIR_ROWS, 512), f32),
            pltpu.VMEM((2, PAIR_ROWS, 512), f32),
            pltpu.VMEM((2, PAIR_ROWS, 512), f32),
            pltpu.VMEM((4, PAIR_ROWS, 128), f32),
            pltpu.VMEM((8, PAIR_ROWS, 128), f32),
            pltpu.VMEM((4, PAIR_ROWS, 128), f32),
            pltpu.VMEM((2, 4, PAIR_ROWS, 128), f32),
            pltpu.VMEM((2, 4, PAIR_ROWS, 128), f32),
            pltpu.VMEM((2, 4, PAIR_ROWS, 128), f32),
            pltpu.VMEM((8, PAIR_ROWS, 128), f32),
            pltpu.VMEM((8, PAIR_ROWS, 128), f32),
            pltpu.VMEM((PAIR_ROWS, 128), f32),
            pltpu.VMEM((PAIR_ROWS, 128), f32),
            pltpu.VMEM((PAIR_ROWS, 128), f32),
            pltpu.VMEM((32, 32, 128), f32),
            pltpu.VMEM((8, 2, 128), f32),
            pltpu.VMEM((8, 2, 128), f32),
            pltpu.VMEM((16, 2, 128), f32),
            dma((5,)), dma((2,)), dma((2,)), dma((8,)), dma((8,)), dma((8,)), dma((8,)), dma((4,)), dma((4,)),
            dma((6,)), dma((6,)), dma((8,)), dma((8,)), dma((1,)), dma((1,)), dma((8,)), dma((8,)),
            dma((8,)), dma((8,)), dma((8,)), dma((8,)), dma((8,)), dma((8,)), dma((16,)), dma((16,)),
        ],
        compiler_params=pltpu.CompilerParams(
            collective_id=0, has_side_effects=True, vmem_limit_bytes=32 * 1024 * 1024
        ),
        name="direct_term",
    )(*(pltpu.with_memory_space_constraint(a, pltpu.HBM) for a in (
        trials, valence_factor.reshape(512, 256), conduction_factor.reshape(2048, 512),
        val_energy.reshape(1, 32), cond_energy.reshape(1, 128),
    )))
    return (applied, residual, quotient.reshape(32))


def solution(mesh):
    split = Mesh(
        mesh.devices.reshape(8, 2, 2, mesh.shape["trial"], mesh.shape["val"]),
        ("x", "zh", "core", "trial", "val"),
    )
    in_specs = (P(None, None, "trial"), P(BLK, "val", None), P(BLK, "trial", None), P("val"), P("trial"))
    out_specs = (P(None, "val", "trial"), P(None, "val", "trial"), P())
    return jax.shard_map(on_device, mesh=split, in_specs=in_specs, out_specs=out_specs, check_vma=False)
```

```python
import jax
import jax.numpy as jnp
from jax import lax
from jax.experimental import pallas as pl
from jax.experimental.pallas import tpu as pltpu
from jax.sharding import Mesh
from jax.sharding import PartitionSpec as P

BLK = ("x", "zh", "core")
MESH = pl.DeviceIdType.MESH
RING = 8
PAIR_ROWS = 64
TARGET = (4, 3, 5, 2, 6, 1, 7, 0)
FAR_FIRST = (4, 3, 5, 2, 6, 1, 7)


def ring(i):
    return lax.rem(i, RING)


def kernel(
    trials_hbm, valence_hbm, conduction_hbm, val_hbm, cond_hbm,
    applied_ref, residual_ref, quotient_ref,
    trials, valence, conduction, val_ref, cond_ref, left, outgoing, from_core, own,
    from_4, from_3, from_2, from_1, blocks, from_z, vectors,
    below, above, beyond, part, from_x, half, other_half, whole,
    gathered, sums_y, sums_z, sums_x,
    load_sem, core_send, core_recv, a_send, a_recv, z_send, z_recv, t_send, t_recv,
    b_send, b_recv, x_send, x_recv, h_send, h_recv, g_send, g_recv, f_send, f_recv,
    qy_send, qy_recv, qz_send, qz_recv, qx_send, qx_recv,
):
    x, zh, core = lax.axis_index("x"), lax.axis_index("zh"), lax.axis_index("core")
    zl, y = lax.axis_index("trial"), lax.axis_index("val")
    z = zh * 4 + zl
    other = 1 - core

    def at_x(step, c):
        return {"x": ring(x + step), "zh": zh, "core": c, "trial": zl, "val": y}

    def at_z(step):
        there = ring(z + step)
        return {"x": x, "zh": there // 4, "core": core, "trial": lax.rem(there, 4), "val": y}

    def at_y(step):
        return {"x": x, "zh": zh, "core": core, "trial": zl, "val": ring(y + step)}

    def remote(src, dst, send, recv, device):
        return pltpu.make_async_remote_copy(
            src_ref=src, dst_ref=dst, send_sem=send, recv_sem=recv,
            device_id=device, device_id_type=MESH,
        )

    loads = [
        pltpu.make_async_copy(src, dst, load_sem.at[i])
        for i, (src, dst) in enumerate((
            (valence_hbm, valence), (trials_hbm, trials), (conduction_hbm, conduction),
            (val_hbm, val_ref), (cond_hbm, cond_ref),
        ))
    ]
    for load in loads:
        load.start()
    barrier = pltpu.get_barrier_semaphore()
    partners = [at_x(0, other)]
    for step in range(1, RING):
        partners += [at_x(step, core), at_x(step, other), at_z(step), at_y(step)]
    for device in partners:
        pl.semaphore_signal(barrier, inc=1, device_id=device, device_id_type=MESH)
    loads[0].wait()
    loads[1].wait()

    def unit(side, u):
        for q in range(4):
            first = 16 * side + 2 * ring(x + TARGET[4 * u + q])
            pair = jnp.concatenate([trials[first], trials[first + 1]], axis=1)
            inner = jnp.dot(valence[...], pair, preferred_element_type=jnp.float32)
            inner = inner.astype(jnp.bfloat16)
            for p in range(16):
                for i in range(2):
                    left[q * 64 + i * 32:q * 64 + i * 32 + 32, p * 128:(p + 1) * 128] = (
                        inner[p * 32:(p + 1) * 32, i * 128:(i + 1) * 128]
                    )
        if side is other and u == 0:
            loads[2].wait()
        return jnp.dot(left[...], conduction[...], preferred_element_type=jnp.float32)

    mine = core * 16 + x * 2
    v_rows = pl.ds(pl.multiple_of(y * 32, 32), 32)
    for i in range(2):
        vectors[0, i * 32:(i + 1) * 32] = trials[mine + i, v_rows, :].astype(jnp.float32)

    def trial_copies():
        return [
            remote(vectors.at[0], vectors.at[slot], t_send.at[slot], t_recv.at[slot], at_z(step))
            for step, slot in ((1, 3), (7, 1), (2, 2))
        ]

    def along_x(kind, way, s):
        n = (kind * 2 + way) * 2 + s
        slot = ((0, 0), (1, 2), (3, 4), (5, 6))[kind][way]
        rows = pl.ds(32 * s, 32)
        dst = (from_4, from_3, from_2, from_1)[kind].at[way, rows]
        reach = (2, 1, 2, 1)[kind]
        return remote(own.at[slot, rows], dst, a_send.at[n], a_recv.at[n], at_x((reach, RING - reach)[way], core))

    along_x_all = [(kind, way, s) for kind in range(4) for way in range(2) for s in range(2) if kind or s == way]

    def block_of(step, u):
        column = pl.multiple_of(lax.rem(zl + step, 4) * 128, 128)
        return own.at[pl.ds(4 * u, 4), pl.ds(0, PAIR_ROWS), pl.ds(column, 128)]

    def along_z(u):
        far = (2, 6)[u]
        return [
            remote(block_of(far, u), beyond.at[u], b_send.at[4 + u], b_recv.at[4 + u], at_z(far)),
            remote(block_of(1, u), below.at[u], b_send.at[u], b_recv.at[u], at_z(1)),
            remote(block_of(7, u), above.at[u], b_send.at[2 + u], b_recv.at[2 + u], at_z(7)),
        ]

    to_core = []
    for u in range(2):
        outgoing[u] = unit(other, u)
        if u == 0:
            pl.semaphore_wait(barrier, len(partners))
        copy = remote(outgoing.at[u], from_core.at[u], core_send.at[u], core_recv.at[u], at_x(0, other))
        copy.start()
        to_core.append(copy)
        if u == 0:
            @pl.when(core == 0)
            def _():
                for copy in trial_copies():
                    copy.start()
        product = unit(core, u)
        to_core[u].wait_recv()
        for q in range(4):
            own[4 * u + q] = product[q * 64:(q + 1) * 64] + from_core[u, q * 64:(q + 1) * 64]

        @pl.when(core == 0)
        def _():
            if u == 0:
                for way in range(2):
                    along_x(0, way, way).start()
                for way in range(2):
                    along_x(1, way, 1 - way).start()
                for way in range(2):
                    along_x(1, way, way).start()
            else:
                for way in range(2):
                    for s in range(2):
                        along_x(3, way, s).start()
                for way in range(2):
                    s, slot, rows = 1 - way, 3 + way, slice(32 - 32 * way, 64 - 32 * way)
                    along_x(1, way, s).wait_recv()
                    own[slot, rows] = own[slot, rows] + from_3[way, rows]
                    along_x(2, way, s).start()
                for way in range(2):
                    s, slot, rows = way, 3 + way, slice(32 * way, 32 * way + 32)
                    along_x(1, way, s).wait_recv()
                    along_x(0, way, s).wait_recv()
                    own[slot, rows] = own[slot, rows] + from_3[way, rows] + from_4[way, rows]
                    along_x(2, way, s).start()

        @pl.when(core == 1)
        def _():
            for copy in along_z(u):
                copy.start()

    loads[3].wait()
    loads[4].wait()
    on_diagonal = lax.broadcasted_iota(jnp.int32, (32, 128), 0) == lax.broadcasted_iota(jnp.int32, (32, 128), 1)
    val_row = jnp.concatenate([val_ref[...], jnp.zeros((1, 96), jnp.float32)], axis=1)
    energy = cond_ref[...] - jnp.sum(jnp.where(on_diagonal, val_row, 0.0), axis=1, keepdims=True)

    def in_lanes(values, first):
        count = values.shape[0]
        column = jnp.sum(values, axis=1, keepdims=True)
        lane = lax.broadcasted_iota(jnp.int32, (count, 128), 1)
        row = lax.broadcasted_iota(jnp.int32, (count, 128), 0)
        return jnp.sum(jnp.where(lane == row + first, column, 0.0), axis=0, keepdims=True)

    def over_rows(values):
        return jnp.sum(values, axis=0, keepdims=True)

    fixed, squares = [], []
    for i in range(2):
        vector = vectors[0, i * 32:(i + 1) * 32]
        square = jnp.where(zh == 0, vector * vector, 0.0)
        fixed.append(over_rows(energy * square))
        squares.append(over_rows(square))
    fixed = in_lanes(jnp.concatenate(fixed, axis=0), mine)
    sums_y[0, 1:2] = in_lanes(jnp.concatenate(squares, axis=0), mine)

    def z_copy(step):
        return remote(blocks.at[lax.rem(zl + step, 4)], from_z.at[step], z_send.at[step], z_recv.at[step], at_z(step))

    def x_copy(step):
        return remote(part.at[ring(x + step)], from_x.at[step], x_send.at[step], x_recv.at[step], at_x(step, core))

    def half_copy():
        return remote(half, other_half, h_send.at[0], h_recv.at[0], at_z(4))

    @pl.when(core == 0)
    def _():
        for kind in (3, 2):
            for way in range(2):
                for s in range(2):
                    along_x(kind, way, s).wait_recv()
        summed = own[7] + from_1[0] + from_1[1] + from_2[0] + from_2[1]
        for b in range(4):
            blocks[b] = summed[:, b * 128:(b + 1) * 128]
        for step in FAR_FIRST:
            z_copy(step).start()
        from_z[0] = blocks[zl]
        for copy in trial_copies():
            copy.wait_recv()
        products = []
        for i in range(2):
            rows = slice(i * 32, (i + 1) * 32)
            product = vectors[0, rows] * blocks[zl, rows]
            for b in range(1, 4):
                product = product + vectors[b, rows] * blocks[lax.rem(zl + b, 4), rows]
            products.append(over_rows(product))
        sums_y[0, 0:1] = fixed + in_lanes(jnp.concatenate(products, axis=0), mine)

    @pl.when(core == 1)
    def _():
        products = [None] * 16
        column = pl.ds(pl.multiple_of(zl * 128, 128), 128)
        for u in range(2):
            for copy in along_z(u):
                copy.wait_recv()
            for q in range(4):
                k = 4 * u + q
                part[ring(x + TARGET[k])] = own[k, :, column] + below[u, q] + above[u, q] + beyond[u, q]
                if TARGET[k]:
                    x_copy(TARGET[k]).start()
        for t in range(16):
            image = part[t // 2, (t % 2) * 32:(t % 2) * 32 + 32]
            products[t] = over_rows(image * trials[16 + t, v_rows, :].astype(jnp.float32))
        sums_y[0, 0:1] = fixed + in_lanes(jnp.concatenate(products, axis=0), 16)

    y_copies = []
    for step in FAR_FIRST:
        copy = remote(sums_y.at[0], sums_y.at[step], qy_send.at[step], qy_recv.at[step], at_y(step))
        copy.start()
        y_copies.append(copy)

    @pl.when(core == 1)
    def _():
        total = part[x]
        for step in FAR_FIRST:
            x_copy(step).wait_recv()
            total = total + from_x[step]
        half[...] = total
        half_copy().start()

    for copy in y_copies:
        copy.wait_recv()
    total = sums_y[ring(y + RING)]
    for i in range(1, RING):
        total = total + sums_y[ring(y + RING - i)]
    sums_z[0] = total
    q_copies = []
    for step in FAR_FIRST:
        copy = remote(sums_z.at[0], sums_z.at[step], qz_send.at[step], qz_recv.at[step], at_z(step))
        copy.start()
        q_copies.append(copy)

    @pl.when(core == 0)
    def _():
        for step in reversed(FAR_FIRST):
            z_copy(step).wait_recv()
        total = from_z[ring(z + RING)]
        for i in range(1, RING):
            total = total + from_z[ring(z + RING - i)]
        whole[...] = total

    @pl.when(core == 1)
    def _():
        half_copy().wait_recv()
        whole[...] = half[...] + other_half[...]

    for i in range(2):
        rows = slice(i * 32, (i + 1) * 32)
        gathered[mine + i] = whole[rows] + energy * vectors[0, rows]
    g_copies = {}
    pair = pl.ds(mine, 2)
    for step in FAR_FIRST:
        copy = remote(gathered.at[pair], gathered.at[pair], g_send.at[step], g_recv.at[step], at_x(step, core))
        copy.start()
        g_copies[step] = copy
    f_copies = {}

    def forward(step):
        there = pl.ds(core * 16 + 2 * ring(x + RING - step), 2)
        if step:
            g_copies[step].wait_recv()
        copy = remote(gathered.at[there], gathered.at[there], f_send.at[step], f_recv.at[step], at_x(0, other))
        copy.start()
        f_copies[step] = copy

    forward(0)
    for copy in q_copies:
        copy.wait_recv()
    total = sums_z[ring(z + RING)]
    for i in range(1, RING):
        total = total + sums_z[ring(z + RING - i)]
    seat = core * 8 + x
    sums_x[seat] = total
    seat_copies = []
    for n in list(range(2, 16)) + [1]:
        step, c = n // 2, (core if n % 2 == 0 else other)
        copy = remote(sums_x.at[seat], sums_x.at[seat], qx_send.at[n], qx_recv.at[n], at_x(step, c))
        copy.start()
        seat_copies.append(copy)
    for step in reversed(FAR_FIRST):
        forward(step)
    for copy in seat_copies:
        copy.wait_recv()
    total = sums_x[0]
    for n in range(1, 16):
        total = total + sums_x[n]
    ratio = total[0:1] / (total[1:2] + 1e-6)
    quotient_ref[...] = ratio[:, 0:32]
    quotients = jnp.sum(jnp.where(on_diagonal, ratio, 0.0), axis=1, keepdims=True)
    for step in range(RING):
        f_copies[step].wait_recv()
    for t in range(32):
        image = gathered[t]
        applied_ref[t] = image
        residual_ref[t] = image - quotients[t:t + 1, :] * trials[t, v_rows, :].astype(jnp.float32)

    @pl.when(core == 0)
    def _():
        for copy in trial_copies():
            copy.wait_send()
        for kind, way, s in along_x_all:
            along_x(kind, way, s).wait_send()
        for step in FAR_FIRST:
            z_copy(step).wait_send()

    @pl.when(core == 1)
    def _():
        for u in range(2):
            for copy in along_z(u):
                copy.wait_send()
        for step in FAR_FIRST:
            x_copy(step).wait_send()
        half_copy().wait_send()

    for group in (to_core, g_copies.values(), f_copies.values(), y_copies, q_copies, seat_copies):
        for copy in group:
            copy.wait_send()


def write_out(applied, residual, quotient, applied_hbm, residual_hbm, quotient_hbm, sems):
    copies = [
        pltpu.make_async_copy(src, dst, sems.at[i])
        for i, (src, dst) in enumerate((
            (applied, applied_hbm), (residual, residual_hbm), (quotient, quotient_hbm),
        ))
    ]
    for copy in copies:
        copy.start()
    for copy in copies:
        copy.wait()


def on_device(trials, valence_factor, conduction_factor, val_energy, cond_energy):
    vmem = pl.BlockSpec(memory_space=pltpu.VMEM)
    hbm = pl.BlockSpec(memory_space=pltpu.HBM)
    dma = pltpu.SemaphoreType.DMA
    f32 = jnp.float32
    applied, residual, quotient = pl.pallas_call(
        kernel,
        out_shape=(
            jax.ShapeDtypeStruct((32, 32, 128), f32),
            jax.ShapeDtypeStruct((32, 32, 128), f32),
            jax.ShapeDtypeStruct((1, 32), f32),
        ),
        in_specs=[hbm] * 5,
        out_specs=(vmem, vmem, vmem),
        scratch_shapes=[
            pltpu.VMEM((32, 256, 128), jnp.bfloat16),
            pltpu.VMEM((512, 256), jnp.bfloat16),
            pltpu.VMEM((2048, 512), jnp.bfloat16),
            pltpu.VMEM((1, 32), f32),
            pltpu.VMEM((1, 128), f32),
            pltpu.VMEM((256, 2048), jnp.bfloat16),
            pltpu.VMEM((2, 256, 512), f32),
            pltpu.VMEM((2, 256, 512), f32),
            pltpu.VMEM((8, PAIR_ROWS, 512), f32),
            pltpu.VMEM((2, PAIR_ROWS, 512), f32),
            pltpu.VMEM((2, PAIR_ROWS, 512), f32),
            pltpu.VMEM((2, PAIR_ROWS, 512), f32),
            pltpu.VMEM((2, PAIR_ROWS, 512), f32),
            pltpu.VMEM((4, PAIR_ROWS, 128), f32),
            pltpu.VMEM((8, PAIR_ROWS, 128), f32),
            pltpu.VMEM((4, PAIR_ROWS, 128), f32),
            pltpu.VMEM((2, 4, PAIR_ROWS, 128), f32),
            pltpu.VMEM((2, 4, PAIR_ROWS, 128), f32),
            pltpu.VMEM((2, 4, PAIR_ROWS, 128), f32),
            pltpu.VMEM((8, PAIR_ROWS, 128), f32),
            pltpu.VMEM((8, PAIR_ROWS, 128), f32),
            pltpu.VMEM((PAIR_ROWS, 128), f32),
            pltpu.VMEM((PAIR_ROWS, 128), f32),
            pltpu.VMEM((PAIR_ROWS, 128), f32),
            pltpu.VMEM((32, 32, 128), f32),
            pltpu.VMEM((8, 2, 128), f32),
            pltpu.VMEM((8, 2, 128), f32),
            pltpu.VMEM((16, 2, 128), f32),
            dma((5,)), dma((2,)), dma((2,)), dma((16,)), dma((16,)), dma((8,)), dma((8,)), dma((4,)), dma((4,)),
            dma((6,)), dma((6,)), dma((8,)), dma((8,)), dma((1,)), dma((1,)), dma((8,)), dma((8,)),
            dma((8,)), dma((8,)), dma((8,)), dma((8,)), dma((8,)), dma((8,)), dma((16,)), dma((16,)),
        ],
        compiler_params=pltpu.CompilerParams(
            collective_id=0, has_side_effects=True, vmem_limit_bytes=32 * 1024 * 1024
        ),
        name="direct_term",
    )(*(pltpu.with_memory_space_constraint(a, pltpu.HBM) for a in (
        trials, valence_factor.reshape(512, 256), conduction_factor.reshape(2048, 512),
        val_energy.reshape(1, 32), cond_energy.reshape(1, 128),
    )))
    applied, residual, quotient = pl.pallas_call(
        write_out,
        out_shape=(
            jax.ShapeDtypeStruct((32, 32, 128), f32),
            jax.ShapeDtypeStruct((32, 32, 128), f32),
            jax.ShapeDtypeStruct((1, 32), f32),
        ),
        in_specs=[vmem] * 3,
        out_specs=(hbm, hbm, hbm),
        scratch_shapes=[dma((3,))],
        compiler_params=pltpu.CompilerParams(vmem_limit_bytes=1024 * 1024),
        name="write_out",
    )(applied, residual, quotient)
    return (applied, residual, quotient.reshape(32))


def solution(mesh):
    split = Mesh(
        mesh.devices.reshape(8, 2, 2, mesh.shape["trial"], mesh.shape["val"]),
        ("x", "zh", "core", "trial", "val"),
    )
    in_specs = (P(None, None, "trial"), P(BLK, "val", None), P(BLK, "trial", None), P("val"), P("trial"))
    out_specs = (P(None, "val", "trial"), P(None, "val", "trial"), P())
    return jax.shard_map(on_device, mesh=split, in_specs=in_specs, out_specs=out_specs, check_vma=False)
```
